32 devices in a mesh: area: 8 (over z, x), scen: 4 (over y, core).
Axes of the slice: x: 2, y: 2, z: 4, core: 2. Of those that a mesh axis runs over, the one named last changes fastest.
Arguments:
- injection: float32 [8, 128, 4096], P('area', 'scen'), may hold values from -6 to 6
- kkt_factor: bfloat16 [8, 4096, 4096], P('area', 'scen'), may hold values from -0.09375 to 0.09375
- dual_price: float32 [8, 128, 512], P('area', 'scen'), may hold values from -6 to 6
- area_size: int32 [8], replicated, may hold values from 1024 to 4096, as said below
- bnd_bus: int32 [8, 512], replicated, may hold values from 0 to 4095, as said below
- peer_end: int32 [8, 512], replicated, may hold values from 0 to 4095, as said below
Outputs:
- angles: float32 [8, 128, 4096], P('area', 'scen')
- dual_out: float32 [8, 128, 512], P('area', 'scen')
- consensus: float32 [8, 128, 512], P('area', 'scen')
The draws below stay inside these ranges and needn't reach their ends.
Inputs may be any that keep to these rules, and one draw needn't show every extreme that they name: `area_size`: one area has exactly 4096 live buses and another exactly 1024. `bnd_bus`: the buses of one area's ends are distinct and lie below that area's size; they include bus 0 and the area's last live bus. peer_end is a pairing: the peer of an end's peer is the end itself, and the two ends lie in different areas. The ends of area a form 4 tie sets of 128 consecutive ends; tie set g of area a is paired whole with tie set g of area a XOR s_g, where s_g is nonzero, the same for all areas, and the 4 values s_g differ.
All inputs are finite; a program needn't handle non-finite values.
Results may differ from the reference program's by a relative error of at most 0.0043.
Values may be sent and summed in bfloat16 or wider, within the bound.
No kernel may reach another device: no remote copies, remote signals or barrier semaphores. Data moves between devices by JAX's collectives and lax.ppermute only.
A program may use at most 128 MiB of HBM per device.

```python
import jax
import jax.numpy as jnp
from jax import lax

NB = 4096
NBND = 512
CAP = 128
NGRP = 4
COLS = 128
AREAS = 8
ITERS = 2


def sizes_table(key):
    sub_key = jax.random.fold_in(key, 11)
    first_key, second_key = jax.random.split(sub_key)
    drawn = jax.random.randint(first_key, (AREAS,), NB // 4, NB + 1)
    chosen = jax.random.randint(second_key, (), 0, AREAS)
    drawn = drawn.at[(chosen + 1) % AREAS].set(NB // 4)
    return drawn.at[chosen].set(NB)


def bus_order(one_key):
    return jax.random.permutation(one_key, NB)


def slot_order(one_key):
    return jax.random.permutation(one_key, CAP)


def draw_area_size(key, part):
    return sizes_table(key).astype(jnp.int32)


def draw_bnd_bus(key, part):
    sizes = sizes_table(key)
    keys_all = jax.random.split(jax.random.fold_in(key, 13), AREAS)
    ranks = jax.vmap(bus_order)(keys_all)
    bus_ids = jnp.arange(NB)[None, :]
    scores = ranks + jnp.where(bus_ids >= sizes[:, None], NB, 0)
    scores = jnp.where(bus_ids == 0, -2, jnp.where(bus_ids == sizes[:, None] - 1, -1, scores))
    return jnp.argsort(scores, axis=1)[:, :NBND].astype(jnp.int32)


def draw_peer_end(key, part):
    base_key = jax.random.fold_in(key, 17)
    shift_key, perm_key = jax.random.split(base_key)
    shifts = jax.random.permutation(shift_key, AREAS - 1)[:NGRP] + 1
    perms = jax.vmap(slot_order)(jax.random.split(perm_key, AREAS * NGRP)).reshape(AREAS, NGRP, CAP)
    inverse = jnp.argsort(perms, axis=-1)
    area_ids = jnp.arange(AREAS)[:, None]
    group_ids = jnp.arange(NGRP)[None, :]
    partner = jnp.bitwise_xor(area_ids, shifts[None, :])
    lower_side = (area_ids < partner)[:, :, None]
    own_perm = perms[area_ids, group_ids]
    other_inverse = inverse[partner, group_ids]
    slots = jnp.where(lower_side, own_perm, other_inverse)
    peers = partner[:, :, None] * NBND + group_ids[:, :, None] * CAP + slots
    return peers.reshape(AREAS, NBND).astype(jnp.int32)


def block_levels(own_key, dims, cuts, least, high):
    level = 1.0
    for axis_at, parts in cuts:
        steps = jax.random.uniform(jax.random.fold_in(jax.random.fold_in(own_key, 6), axis_at), (parts,), jnp.float32, least / len(cuts), high / len(cuts))
        level = level * jnp.repeat(jnp.exp(steps), dims[axis_at] // parts).reshape((-1,) + (1,) * (len(dims) - 1 - axis_at))
    return level


def noise(rng, dims, scale, most, cuts=(), kind=jnp.bfloat16):
    values = scale * jax.random.normal(rng, dims, jnp.float32)
    if cuts:
        values = values * block_levels(rng, dims, cuts, -0.22, 0.18)
    return jnp.clip(values, -most, most).astype(kind)


def setup_inputs(seed: int = 0) -> dict:
    key_of = jax.random.split(jax.random.key(seed), 7)
    injection = noise(key_of[0], (AREAS, COLS, NB), 1.0, 6.0, ((0, 8), (1, 4)), jnp.float32)
    kkt_factor = noise(key_of[1], (AREAS, NB, NB), NB ** -0.5, 0.09375, ((0, 8), (1, 4)))
    dual_price = noise(key_of[2], (AREAS, COLS, NBND), 1.0, 6.0, ((0, 8), (1, 4)), jnp.float32)
    area_size = draw_area_size(jax.random.fold_in(key_of[6], 71), 0)
    bnd_bus = draw_bnd_bus(jax.random.fold_in(key_of[6], 71), 0)
    peer_end = draw_peer_end(jax.random.fold_in(key_of[6], 71), 0)
    return {"injection": injection, "kkt_factor": kkt_factor, "dual_price": dual_price, "area_size": area_size, "bnd_bus": bnd_bus, "peer_end": peer_end}


PENALTY = 1.5
PROXIMAL = 0.5


def scatter_area(values, buses):
    return jnp.zeros((values.shape[0], NB), jnp.float32).at[:, buses].add(values)


def pick_area(angles, buses):
    return angles[:, buses]


def solve_area(operands):
    right_side, factor, live_mask = operands
    projected = jnp.dot(right_side, factor.T, preferred_element_type=jnp.float32)
    projected = (projected * live_mask).astype(jnp.bfloat16)
    return jnp.dot(projected, factor, preferred_element_type=jnp.float32) * live_mask


def mates(values, peer_end):
    flat = jnp.transpose(values, (1, 0, 2)).reshape(values.shape[1], AREAS * NBND)
    taken = flat[:, peer_end.reshape(-1)]
    return jnp.transpose(taken.reshape(values.shape[1], AREAS, NBND), (1, 0, 2))


def reference(injection, kkt_factor, dual_price, area_size, bnd_bus, peer_end):
    live_mask = (jnp.arange(NB)[None, None, :] < area_size[:, None, None]).astype(jnp.float32)
    consensus = jnp.zeros_like(dual_price)
    angles = jnp.zeros_like(injection)
    for sweep in range(ITERS):
        spread = jax.vmap(scatter_area)(dual_price - PENALTY * consensus, bnd_bus)
        right_side = ((injection - spread) * live_mask).astype(jnp.bfloat16)
        angles = lax.map(solve_area, (right_side, kkt_factor, live_mask))
        end_angles = jax.vmap(pick_area)(angles, bnd_bus)
        consensus = (PENALTY * (end_angles + mates(end_angles, peer_end)) + (dual_price + mates(dual_price, peer_end)) + PROXIMAL * consensus) / (2.0 * PENALTY + PROXIMAL)
        dual_price = dual_price + PENALTY * (end_angles - consensus)
    return angles, dual_price, consensus
```

```python
import jax
import jax.numpy as jnp
from jax import lax
from jax.sharding import PartitionSpec as P

CAP = 128
PENALTY = 1.5
PROXIMAL = 0.5
DENOM = 2.0 * PENALTY + PROXIMAL


F32 = jnp.float32
BF16 = jnp.bfloat16


def dot_nt(a, b):
    return lax.dot_general(a, b, (((1,), (1,)), ((), ())), preferred_element_type=F32)


def dot_tn(a, b):
    return lax.dot_general(a, b, (((0,), (0,)), ((), ())), preferred_element_type=F32)


def dot_nn(a, b):
    return jnp.dot(a, b, preferred_element_type=F32)


def swap(x, axis, bit):
    n = lax.axis_size(axis)
    return lax.ppermute(x, axis, [(i, i ^ bit) for i in range(n)])


def halves(x):
    high = x.astype(BF16)
    return high, (x - high.astype(F32)).astype(BF16)


def shards(injection, kkt_factor, dual_price, area_size, bnd_bus, peer_end):
    area_id = lax.axis_index("area")
    band_index = lax.axis_index("scen")
    areas_all = lax.axis_size("area")
    factor = kkt_factor[0]
    band_rows, width = factor.shape
    injection_here = injection[0]
    dual_here = dual_price[0]
    columns, ends_total = dual_here.shape
    size_here = area_size[area_id]
    live_mask = jnp.arange(width) < size_here
    band_mask = band_index * band_rows + jnp.arange(band_rows) < size_here
    buses = bnd_bus[area_id]
    peers = peer_end[area_id]
    offset = (peers // ends_total) ^ area_id

    plain = jnp.where(live_mask, injection_here, 0.0).astype(BF16)
    at_ends = injection_here[:, buses]
    at_ends_high, at_ends_low = halves(at_ends)
    first_here = (at_ends - dual_here).astype(BF16)
    small = jnp.concatenate([first_here, at_ends_high, at_ends_low], axis=1)
    pair = jnp.concatenate([plain, swap(plain, "scen", 2)], axis=0)
    full = jnp.concatenate([pair, swap(pair, "scen", 1)], axis=0)
    small_pair = jnp.concatenate([small, swap(small, "scen", 2)], axis=0)
    small_send = small_pair[:, : 2 * ends_total]
    small_full = jnp.concatenate([small_send, swap(small_send, "scen", 1)], axis=0)
    at_ends_pair = small_pair[:, ends_total : 2 * ends_total].astype(F32)
    at_ends_pair = at_ends_pair + small_pair[:, 2 * ends_total :].astype(F32)

    pick = (jnp.arange(width)[:, None] == buses[None, :]).astype(BF16)
    factor_ends = jnp.where(band_mask[:, None], dot_nn(factor, pick), 0.0).astype(BF16)
    gram = dot_tn(factor_ends, factor_ends)
    slots = jnp.arange(ends_total)
    on_diag = slots[:, None] == slots[None, :]
    squares = jnp.sum(jnp.where(on_diag, gram, 0.0), axis=0, keepdims=True)
    gram = jnp.where(on_diag, 0.0, gram)
    half = ends_total // 2
    side = band_index % 2

    def with_squares(rows, squares):
        high, low = halves(squares)
        blank = jnp.zeros((14, ends_total), BF16)
        return jnp.concatenate([rows.astype(BF16), high, low, blank], axis=0)

    def add_gram(rows, squares, incoming):
        incoming = incoming.astype(F32)
        return rows + incoming[:half], squares + incoming[half : half + 1] + incoming[half + 1 : half + 2]

    gram_keep = lax.dynamic_slice_in_dim(gram, side * half, half, 0)
    gram_send = lax.dynamic_slice_in_dim(gram, (1 - side) * half, half, 0)
    gram_keep, squares = add_gram(
        gram_keep, squares, swap(with_squares(gram_send, squares), "scen", 1)
    )
    gram_keep, squares = add_gram(
        gram_keep, squares, swap(with_squares(gram_keep, squares), "scen", 2)
    )
    gram_keep = gram_keep.astype(BF16)
    gram_other = swap(gram_keep, "scen", 1)
    gram_all = jnp.where(
        side == 0,
        jnp.concatenate([gram_keep, gram_other], axis=0),
        jnp.concatenate([gram_other, gram_keep], axis=0),
    )
    mate = ((slots // CAP * CAP + peers % CAP)[None, :] == slots[:, None]).astype(BF16)

    base = dot_nt(full, factor) - dot_nt(small_full[:, ends_total:], factor_ends)
    base = jnp.where(band_mask[None, :], base, 0.0)
    first = (base + dot_nt(small_full[:, :ends_total], factor_ends)).astype(BF16)
    partial = PENALTY * dot_nn(first, factor_ends)

    def exchange(q):
        moved = q
        bit = 1
        while bit < areas_all:
            moved = jnp.where((offset & bit)[None, :] != 0, swap(moved, "area", bit), moved)
            bit *= 2
        return dot_nn(moved, mate)

    def with_low(x, low_rows):
        high, low = halves(x)
        return jnp.concatenate([high, low[low_rows]], axis=0)

    pair_rows = 2 * columns
    keep = partial[:pair_rows] + swap(partial[pair_rows:], "scen", 1)
    keep = keep + jnp.concatenate([dual_here, jnp.zeros_like(dual_here)], axis=0)
    first_rows, last_rows = slice(0, columns), slice(columns, pair_rows)
    other = swap(with_low(keep, last_rows), "scen", 2).astype(F32)
    q = keep + jnp.concatenate([other[last_rows] + other[pair_rows:], other[first_rows]], axis=0)
    moved = exchange(with_low(q, first_rows))
    moved = jnp.concatenate([moved[first_rows] + moved[pair_rows:], moved[last_rows]], axis=0)
    consensus = (q + moved) / DENOM
    spread = q - 2.0 * PENALTY * consensus
    second_pair = (at_ends_pair - spread).astype(BF16)
    second_full = jnp.concatenate([second_pair, swap(second_pair, "scen", 1)], axis=0)

    q_own, consensus_own = q[:columns], consensus[:columns]
    change = second_pair[:columns].astype(F32) - first_here.astype(F32)
    change_high, change_low = halves(change)
    ends_scaled = (q_own - dual_here) + PENALTY * (
        change * squares + dot_nn(change_high, gram_all) + dot_nn(change_low, gram_all)
    )
    q_last = ends_scaled + (q_own - PENALTY * consensus_own)
    moved = exchange(with_low(q_last, first_rows))
    moved = moved[first_rows] + moved[last_rows]
    consensus_last = (q_last + moved + PROXIMAL * consensus_own) / DENOM
    dual_last = q_last - PENALTY * consensus_last

    second = (base + dot_nt(second_full, factor_ends)).astype(BF16)
    angles = dot_nn(second, factor)
    angles_pair = angles[:pair_rows] + swap(angles[pair_rows:].astype(BF16), "scen", 1).astype(F32)
    angles_here = angles_pair[:columns] + swap(
        angles_pair[columns:].astype(BF16), "scen", 2
    ).astype(F32)
    angles_here = jnp.where(live_mask, angles_here, 0.0)
    return (angles_here[None], dual_last[None], consensus_last[None])


def solution(mesh):
    spec = P("area", "scen", None)
    return jax.shard_map(
        shards,
        mesh=mesh,
        in_specs=(spec, spec, spec, P(), P(), P()),
        out_specs=(spec, spec, spec),
        check_vma=False,
    )
```

```python
import jax
import jax.numpy as jnp
from jax import lax
from jax.experimental import pallas as pl
from jax.experimental.pallas import tpu as pltpu
from jax.sharding import PartitionSpec as P


CAP = 128
PENALTY = 1.5
PROXIMAL = 0.5
DENOM = 2.0 * PENALTY + PROXIMAL
SUBLANES = 16

F32 = jnp.float32
BF16 = jnp.bfloat16

WHOLE = pl.BlockSpec(memory_space=pltpu.VMEM)
SCALARS = pl.BlockSpec(memory_space=pltpu.SMEM)


def dot_nt(a, b):
    return lax.dot_general(a, b, (((1,), (1,)), ((), ())), preferred_element_type=F32)


def dot_tn(a, b):
    return lax.dot_general(a, b, (((0,), (0,)), ((), ())), preferred_element_type=F32)


def dot_nn(a, b):
    return jnp.dot(a, b, preferred_element_type=F32)


def swap(x, axis, bit):
    n = lax.axis_size(axis)
    return lax.ppermute(x, axis, [(i, i ^ bit) for i in range(n)])


def halves(x):
    high = x.astype(BF16)
    return high, (x - high.astype(F32)).astype(BF16)


def out(shape, dtype):
    return jax.ShapeDtypeStruct(shape, dtype)


def live_rows(area_size, band_rows, shape, axis):
    start = lax.axis_index("scen") * band_rows
    return start + lax.broadcasted_iota(jnp.int32, shape, axis) < area_size[lax.axis_index("area")]


def plain_kernel(area_size, injection, plain):
    live = lax.broadcasted_iota(jnp.int32, injection.shape, 1) < area_size[lax.axis_index("area")]
    plain[...] = jnp.where(live, injection[...], 0.0).astype(BF16)


def plain_side(area_size, injection):
    return pl.pallas_call(
        plain_kernel,
        out_shape=out(injection.shape, BF16),
        in_specs=[SCALARS, WHOLE],
        out_specs=WHOLE,
    )(area_size, injection)


def ends_kernel(area_size, bnd_bus, factor, factor_ends, gram, squares, total):
    step = pl.program_id(0)
    rows, depth = factor.shape
    ends_total = bnd_bus.shape[1]

    @pl.when(step == 0)
    def _():
        total[...] = jnp.zeros_like(total)

    buses = bnd_bus[pl.ds(lax.axis_index("area"), 1), :] - step * depth
    pick = lax.broadcasted_iota(jnp.int32, (depth, ends_total), 0) == buses
    total[...] += dot_nn(factor[...], jnp.where(pick, 1.0, 0.0).astype(BF16))

    @pl.when(step == pl.num_programs(0) - 1)
    def _():
        live = live_rows(area_size, rows, total.shape, 0)
        columns = jnp.where(live, total[...], 0.0).astype(BF16)
        factor_ends[...] = columns
        product = dot_tn(columns, columns)
        square = (ends_total, ends_total)
        diag = lax.broadcasted_iota(jnp.int32, square, 0) == lax.broadcasted_iota(
            jnp.int32, square, 1
        )
        squares[...] = jnp.sum(jnp.where(diag, product, 0.0), axis=0, keepdims=True)
        gram[...] = jnp.where(diag, 0.0, product)


def ends_columns(area_size, bnd_bus, factor):
    rows, width = factor.shape
    ends_total = bnd_bus.shape[1]
    depth = 512
    return pl.pallas_call(
        ends_kernel,
        grid=(width // depth,),
        out_shape=(
            out((rows, ends_total), BF16),
            out((ends_total, ends_total), F32),
            out((1, ends_total), F32),
        ),
        in_specs=[SCALARS, WHOLE, pl.BlockSpec((rows, depth), lambda i: (0, i))],
        out_specs=(
            pl.BlockSpec((rows, ends_total), lambda i: (0, 0)),
            pl.BlockSpec((ends_total, ends_total), lambda i: (0, 0)),
            pl.BlockSpec((1, ends_total), lambda i: (0, 0)),
        ),
        scratch_shapes=[pltpu.VMEM((rows, ends_total), F32)],
    )(area_size, bnd_bus, factor)


def base_kernel(
    area_size, near, far, small_near, small_far, factor, factor_ends, base, partial, side, small
):
    step = pl.program_id(0)
    half = near.shape[0]
    ends_total = small.shape[1] // 2

    @pl.when(step == 0)
    def _():
        side[:half] = near[...]
        side[half:] = far[...]
        small[:half] = small_near[...]
        small[half:] = small_far[...]
        partial[...] = jnp.zeros_like(partial)

    here = factor_ends[...]
    value = dot_nt(side[...], factor[...]) - dot_nt(small[:, ends_total:], here)
    start = lax.axis_index("scen") * (pl.num_programs(0) * here.shape[0]) + step * here.shape[0]
    live = start + lax.broadcasted_iota(jnp.int32, value.shape, 1) < area_size[lax.axis_index("area")]
    value = jnp.where(live, value, 0.0)
    base[...] = value
    first = (value + dot_nt(small[:, :ends_total], here)).astype(BF16)
    partial[...] += PENALTY * dot_nn(first, here)


def base_product(area_size, near, far, small_near, small_far, factor, factor_ends):
    rows, width = factor.shape
    ends_total = factor_ends.shape[1]
    count = 2 * near.shape[0]
    block = 256
    return pl.pallas_call(
        base_kernel,
        grid=(rows // block,),
        out_shape=(out((count, rows), F32), out((count, ends_total), F32)),
        in_specs=[
            SCALARS,
            WHOLE,
            WHOLE,
            WHOLE,
            WHOLE,
            pl.BlockSpec((block, width), lambda i: (i, 0)),
            pl.BlockSpec((block, ends_total), lambda i: (i, 0)),
        ],
        out_specs=(
            pl.BlockSpec((count, block), lambda i: (0, i)),
            pl.BlockSpec((count, ends_total), lambda i: (0, 0)),
        ),
        scratch_shapes=[
            pltpu.VMEM((count, width), BF16),
            pltpu.VMEM((count, 2 * ends_total), BF16),
        ],
    )(area_size, near, far, small_near, small_far, factor, factor_ends)


def second_kernel(base, near, far, factor_ends, factor, second, keep, send, right):
    half = near.shape[0]

    @pl.when(pl.program_id(0) == 0)
    def _():
        right[:half] = near[...]
        right[half:] = far[...]
        second[...] = (base[...] + dot_nt(right[...], factor_ends[...])).astype(BF16)

    value = dot_nn(second[...], factor[...])
    keep[...] = value[:half]
    send[...] = value[half:].astype(BF16)


def angles_specs(half, depth, rows, width, parts, part):
    steps = width // parts // depth
    spec = pl.BlockSpec((half, depth), lambda i: (0, i))
    shapes = (out((half, width // parts), F32), out((half, width // parts), BF16))
    return steps, pl.BlockSpec((rows, depth), lambda i: (0, part * steps + i)), spec, shapes


def second_product(base, near, far, factor_ends, factor, parts):
    rows, width = factor.shape
    half = near.shape[0]
    steps, factor_spec, spec, shapes = angles_specs(half, 512, rows, width, parts, 0)
    return pl.pallas_call(
        second_kernel,
        grid=(steps,),
        out_shape=(out((2 * half, rows), BF16),) + shapes,
        in_specs=[WHOLE, WHOLE, WHOLE, WHOLE, factor_spec],
        out_specs=(pl.BlockSpec((2 * half, rows), lambda i: (0, 0)), spec, spec),
        scratch_shapes=[pltpu.VMEM((2 * half, near.shape[1]), BF16)],
    )(base, near, far, factor_ends, factor)


def angles_kernel(second, factor, keep, send):
    half = keep.shape[0]
    value = dot_nn(second[...], factor[...])
    keep[...] = value[:half]
    send[...] = value[half:].astype(BF16)


def angles_product(second, factor, parts, part):
    rows, width = factor.shape
    half = second.shape[0] // 2
    steps, factor_spec, spec, shapes = angles_specs(half, 512, rows, width, parts, part)
    return pl.pallas_call(
        angles_kernel,
        grid=(steps,),
        out_shape=shapes,
        in_specs=[WHOLE, factor_spec],
        out_specs=(spec, spec),
    )(second, factor)


def shards(injection, kkt_factor, dual_price, area_size, bnd_bus, peer_end):
    area_id = lax.axis_index("area")
    band_index = lax.axis_index("scen")
    areas_all = lax.axis_size("area")
    factor = kkt_factor[0]
    _, width = factor.shape
    injection_here = injection[0]
    dual_here = dual_price[0]
    columns, ends_total = dual_here.shape
    buses = bnd_bus[area_id]
    peers = peer_end[area_id]
    offset = (peers // ends_total) ^ area_id

    plain = plain_side(area_size, injection_here)
    other = swap(plain, "scen", 2)
    pair = jnp.concatenate([plain, other], axis=0)
    pair_far = swap(pair, "scen", 1)
    at_ends = injection_here[:, buses]
    at_ends_high, at_ends_low = halves(at_ends)
    first_here = (at_ends - dual_here).astype(BF16)
    small = jnp.concatenate([first_here, at_ends_high, at_ends_low], axis=1)
    small_pair = jnp.concatenate([small, swap(small, "scen", 2)], axis=0)
    small_send = small_pair[:, : 2 * ends_total]
    small_far = swap(small_send, "scen", 1)
    at_ends_pair = small_pair[:, ends_total : 2 * ends_total].astype(F32)
    at_ends_pair = at_ends_pair + small_pair[:, 2 * ends_total :].astype(F32)

    factor_ends, gram, squares = ends_columns(area_size, bnd_bus, factor)
    slots = jnp.arange(ends_total)
    half = ends_total // 2
    side = band_index % 2

    def with_squares(rows, squares):
        high, low = halves(squares)
        blank = jnp.zeros((SUBLANES - 2, ends_total), BF16)
        return jnp.concatenate([rows.astype(BF16), high, low, blank], axis=0)

    def add_gram(rows, squares, incoming):
        incoming = incoming.astype(F32)
        return rows + incoming[:half], squares + incoming[half : half + 1] + incoming[half + 1 : half + 2]

    gram_keep = lax.dynamic_slice_in_dim(gram, side * half, half, 0)
    gram_send = lax.dynamic_slice_in_dim(gram, (1 - side) * half, half, 0)
    gram_keep, squares = add_gram(
        gram_keep, squares, swap(with_squares(gram_send, squares), "scen", 1)
    )
    gram_keep, squares = add_gram(
        gram_keep, squares, swap(with_squares(gram_keep, squares), "scen", 2)
    )
    gram_keep = gram_keep.astype(BF16)
    gram_other = swap(gram_keep, "scen", 1)
    gram_all = jnp.where(
        side == 0,
        jnp.concatenate([gram_keep, gram_other], axis=0),
        jnp.concatenate([gram_other, gram_keep], axis=0),
    )
    mate = ((slots // CAP * CAP + peers % CAP)[None, :] == slots[:, None]).astype(BF16)

    base, partial = base_product(
        area_size, pair, pair_far, small_send, small_far, factor, factor_ends
    )

    def exchange(q):
        moved = q
        bit = 1
        while bit < areas_all:
            moved = jnp.where((offset & bit)[None, :] != 0, swap(moved, "area", bit), moved)
            bit *= 2
        return dot_nn(moved, mate)

    def with_low(x, low_rows):
        high, low = halves(x)
        return jnp.concatenate([high, low[low_rows]], axis=0)

    pair_rows = 2 * columns
    keep = partial[:pair_rows] + swap(partial[pair_rows:], "scen", 1)
    keep = keep + jnp.concatenate([dual_here, jnp.zeros_like(dual_here)], axis=0)
    first_rows, last_rows = slice(0, columns), slice(columns, pair_rows)
    other = swap(with_low(keep, last_rows), "scen", 2).astype(F32)
    q = keep + jnp.concatenate([other[last_rows] + other[pair_rows:], other[first_rows]], axis=0)
    moved = exchange(with_low(q, first_rows))
    moved = jnp.concatenate([moved[first_rows] + moved[pair_rows:], moved[last_rows]], axis=0)
    consensus = (q + moved) / DENOM
    spread = q - 2.0 * PENALTY * consensus
    second_pair = (at_ends_pair - spread).astype(BF16)
    second_far = swap(second_pair, "scen", 1)

    q_own, consensus_own = q[:columns], consensus[:columns]
    change = second_pair[:columns].astype(F32) - first_here.astype(F32)
    change_high, change_low = halves(change)
    ends_scaled = (q_own - dual_here) + PENALTY * (
        change * squares + dot_nn(change_high, gram_all) + dot_nn(change_low, gram_all)
    )
    q_last = ends_scaled + (q_own - PENALTY * consensus_own)
    moved = exchange(with_low(q_last, first_rows))
    moved = moved[first_rows] + moved[last_rows]
    consensus_last = (q_last + moved + PROXIMAL * consensus_own) / DENOM
    dual_last = q_last - PENALTY * consensus_last

    parts = 2
    second, keep, send = second_product(base, second_pair, second_far, factor_ends, factor, parts)
    pieces = []
    for part in range(parts):
        if part:
            keep, send = angles_product(second, factor, parts, part)
        keep = keep + swap(send, "scen", 1).astype(F32)
        pieces.append(keep[:columns] + swap(keep[columns:].astype(BF16), "scen", 2).astype(F32))
    live_mask = jnp.arange(width) < area_size[area_id]
    angles_here = jnp.where(live_mask, jnp.concatenate(pieces, axis=1), 0.0)
    return (angles_here[None], dual_last[None], consensus_last[None])


def solution(mesh):
    spec = P("area", "scen", None)
    return jax.shard_map(
        shards,
        mesh=mesh,
        in_specs=(spec, spec, spec, P(), P(), P()),
        out_specs=(spec, spec, spec),
        check_vma=False,
    )
```

```python
import jax
import jax.numpy as jnp
from jax import lax
from jax.experimental import pallas as pl
from jax.experimental.pallas import tpu as pltpu
from jax.sharding import PartitionSpec as P


CAP = 128
PENALTY = 1.5
PROXIMAL = 0.5
DENOM = 2.0 * PENALTY + PROXIMAL
SUBLANES = 16

F32 = jnp.float32
BF16 = jnp.bfloat16

WHOLE = pl.BlockSpec(memory_space=pltpu.VMEM)
SCALARS = pl.BlockSpec(memory_space=pltpu.SMEM)


def dot_nt(a, b):
    return lax.dot_general(a, b, (((1,), (1,)), ((), ())), preferred_element_type=F32)


def dot_tn(a, b):
    return lax.dot_general(a, b, (((0,), (0,)), ((), ())), preferred_element_type=F32)


def dot_nn(a, b):
    return jnp.dot(a, b, preferred_element_type=F32)


def swap(x, axis, bit):
    n = lax.axis_size(axis)
    return lax.ppermute(x, axis, [(i, i ^ bit) for i in range(n)])


def halves(x):
    high = x.astype(BF16)
    return high, (x - high.astype(F32)).astype(BF16)


def out(shape, dtype):
    return jax.ShapeDtypeStruct(shape, dtype)


def plain_kernel(area_size, injection, dual, packed):
    width = injection.shape[1]
    live = lax.broadcasted_iota(jnp.int32, injection.shape, 1) < area_size[lax.axis_index("area")]
    packed[:, :width] = jnp.where(live, injection[...], 0.0).astype(BF16)
    packed[:, width:] = dual[...].astype(BF16)


def packed_side(area_size, injection, dual):
    return pl.pallas_call(
        plain_kernel,
        out_shape=out((injection.shape[0], injection.shape[1] + dual.shape[1]), BF16),
        in_specs=[SCALARS, WHOLE, WHOLE],
        out_specs=WHOLE,
    )(area_size, injection, dual)


def base_kernel(area_size, near, far, dual, factor, factor_ends, base, keep, send, side, partial):
    step = pl.program_id(0)
    half = near.shape[0]
    block, width = factor.shape

    @pl.when(step == 0)
    def _():
        side[:half] = near[...]
        side[half:] = far[...]
        partial[...] = jnp.zeros_like(partial)

    here = factor_ends[...]
    value = dot_nt(side[:, :width], factor[...])
    start = lax.axis_index("scen") * (pl.num_programs(0) * block) + step * block
    live = start + lax.broadcasted_iota(jnp.int32, value.shape, 1) < area_size[lax.axis_index("area")]
    value = jnp.where(live, value, 0.0)
    base[...] = value
    first = (value - dot_nt(side[:, width:], here)).astype(BF16)
    partial[...] += dot_nn(first, here)

    @pl.when(step == pl.num_programs(0) - 1)
    def _():
        count = dual.shape[0]
        keep[:count] = PENALTY * partial[:count] + dual[...]
        keep[count:] = PENALTY * partial[count:half]
        send[...] = PENALTY * partial[half:]


def base_product(area_size, near, far, dual, factor, factor_ends):
    rows, width = factor.shape
    half, packed_width = near.shape
    ends_total = factor_ends.shape[1]
    block = 512
    fixed = pl.BlockSpec((half, ends_total), lambda i: (0, 0))
    return pl.pallas_call(
        base_kernel,
        grid=(rows // block,),
        out_shape=(
            out((2 * half, rows), F32),
            out((half, ends_total), F32),
            out((half, ends_total), F32),
        ),
        in_specs=[
            SCALARS,
            WHOLE,
            WHOLE,
            WHOLE,
            pl.BlockSpec((block, width), lambda i: (i, 0)),
            pl.BlockSpec((block, ends_total), lambda i: (i, 0)),
        ],
        out_specs=(pl.BlockSpec((2 * half, block), lambda i: (0, i)), fixed, fixed),
        scratch_shapes=[
            pltpu.VMEM((2 * half, packed_width), BF16),
            pltpu.VMEM((2 * half, ends_total), F32),
        ],
    )(area_size, near, far, dual, factor, factor_ends)


def second_kernel(base, near, far, factor_ends, factor, second, keep, send, right):
    half = near.shape[0]

    @pl.when(pl.program_id(0) == 0)
    def _():
        right[:half] = near[...]
        right[half:] = far[...]
        second[...] = (base[...] - dot_nt(right[...], factor_ends[...])).astype(BF16)

    value = dot_nn(second[...], factor[...])
    keep[...] = value[:half]
    send[...] = value[half:].astype(BF16)


def angles_specs(half, depth, rows, width, parts, part):
    steps = width // parts // depth
    spec = pl.BlockSpec((half, depth), lambda i: (0, i))
    shapes = (out((half, width // parts), F32), out((half, width // parts), BF16))
    return steps, pl.BlockSpec((rows, depth), lambda i: (0, part * steps + i)), spec, shapes


def second_product(base, near, far, factor_ends, factor, parts):
    rows, width = factor.shape
    half = near.shape[0]
    steps, factor_spec, spec, shapes = angles_specs(half, 1024, rows, width, parts, 0)
    return pl.pallas_call(
        second_kernel,
        grid=(steps,),
        out_shape=(out((2 * half, rows), BF16),) + shapes,
        in_specs=[WHOLE, WHOLE, WHOLE, WHOLE, factor_spec],
        out_specs=(pl.BlockSpec((2 * half, rows), lambda i: (0, 0)), spec, spec),
        scratch_shapes=[pltpu.VMEM((2 * half, near.shape[1]), BF16)],
    )(base, near, far, factor_ends, factor)


def angles_kernel(second, factor, keep, send):
    half = keep.shape[0]
    value = dot_nn(second[...], factor[...])
    keep[...] = value[:half]
    send[...] = value[half:].astype(BF16)


def angles_product(second, factor, parts, part):
    rows, width = factor.shape
    half = second.shape[0] // 2
    steps, factor_spec, spec, shapes = angles_specs(half, 1024, rows, width, parts, part)
    return pl.pallas_call(
        angles_kernel,
        grid=(steps,),
        out_shape=shapes,
        in_specs=[WHOLE, factor_spec],
        out_specs=(spec, spec),
    )(second, factor)


def shards(injection, kkt_factor, dual_price, area_size, bnd_bus, peer_end):
    area_id = lax.axis_index("area")
    band_index = lax.axis_index("scen")
    areas_all = lax.axis_size("area")
    factor = kkt_factor[0]
    band_rows, width = factor.shape
    injection_here = injection[0]
    dual_here = dual_price[0]
    columns, ends_total = dual_here.shape
    size_here = area_size[area_id]
    buses = bnd_bus[area_id]
    peers = peer_end[area_id]
    offset = (peers // ends_total) ^ area_id

    packed = packed_side(area_size, injection_here, dual_here)
    other = swap(packed, "scen", 2)
    pair = jnp.concatenate([packed, other], axis=0)
    pair_far = swap(pair, "scen", 1)

    live_band = (band_index * band_rows + jnp.arange(band_rows))[:, None] < size_here
    pick = (jnp.arange(width)[:, None] == buses[None, :]).astype(BF16)
    factor_ends = jnp.where(live_band, dot_nn(factor, pick), 0.0).astype(BF16)
    gram = dot_tn(factor_ends, factor_ends)
    slots = jnp.arange(ends_total)
    on_diag = slots[:, None] == slots[None, :]
    squares = jnp.sum(jnp.where(on_diag, gram, 0.0), axis=0, keepdims=True)
    gram = jnp.where(on_diag, 0.0, gram)
    half = ends_total // 2
    side = band_index % 2

    def with_squares(rows, squares):
        high, low = halves(squares)
        blank = jnp.zeros((SUBLANES - 2, ends_total), BF16)
        return jnp.concatenate([rows.astype(BF16), high, low, blank], axis=0)

    def add_gram(rows, squares, incoming):
        incoming = incoming.astype(F32)
        return rows + incoming[:half], squares + incoming[half : half + 1] + incoming[half + 1 : half + 2]

    gram_keep = lax.dynamic_slice_in_dim(gram, side * half, half, 0)
    gram_send = lax.dynamic_slice_in_dim(gram, (1 - side) * half, half, 0)
    gram_keep, squares = add_gram(
        gram_keep, squares, swap(with_squares(gram_send, squares), "scen", 1)
    )
    gram_keep, squares = add_gram(
        gram_keep, squares, swap(with_squares(gram_keep, squares), "scen", 2)
    )
    gram_keep = gram_keep.astype(BF16)
    gram_other = swap(gram_keep, "scen", 1)
    gram_all = jnp.where(
        side == 0,
        jnp.concatenate([gram_keep, gram_other], axis=0),
        jnp.concatenate([gram_other, gram_keep], axis=0),
    )
    mate = ((slots // CAP * CAP + peers % CAP)[None, :] == slots[:, None]).astype(BF16)

    base, keep, send = base_product(
        area_size, pair, pair_far, dual_here, factor, factor_ends
    )

    def exchange(q):
        moved = q
        bit = 1
        while bit < areas_all:
            moved = jnp.where((offset & bit)[None, :] != 0, swap(moved, "area", bit), moved)
            bit *= 2
        return dot_nn(moved, mate)

    def with_low(x, low_rows):
        high, low = halves(x)
        return jnp.concatenate([high, low[low_rows]], axis=0)

    pair_rows = 2 * columns
    keep = keep + swap(send, "scen", 1)
    pair_rows = 2 * columns
    first_rows, last_rows = slice(0, columns), slice(columns, pair_rows)
    other = swap(with_low(keep, last_rows), "scen", 2).astype(F32)
    q = keep + jnp.concatenate([other[last_rows] + other[pair_rows:], other[first_rows]], axis=0)
    moved = exchange(with_low(q, first_rows))
    moved = jnp.concatenate([moved[first_rows] + moved[pair_rows:], moved[last_rows]], axis=0)
    consensus = (q + moved) / DENOM
    spread = q - 2.0 * PENALTY * consensus
    spread_pair = spread.astype(BF16)
    spread_far = swap(spread_pair, "scen", 1)

    q_own, consensus_own = q[:columns], consensus[:columns]
    change = spread_pair[:columns].astype(F32) - dual_here.astype(BF16).astype(F32)
    change_high, change_low = halves(change)
    ends_scaled = (q_own - dual_here) - PENALTY * (
        change * squares + dot_nn(change_high, gram_all) + dot_nn(change_low, gram_all)
    )
    q_last = ends_scaled + (q_own - PENALTY * consensus_own)
    moved = exchange(with_low(q_last, first_rows))
    moved = moved[first_rows] + moved[last_rows]
    consensus_last = (q_last + moved + PROXIMAL * consensus_own) / DENOM
    dual_last = q_last - PENALTY * consensus_last

    parts = 2
    second, keep, send = second_product(base, spread_pair, spread_far, factor_ends, factor, parts)
    pieces = []
    for part in range(parts):
        if part:
            keep, send = angles_product(second, factor, parts, part)
        keep = keep + swap(send, "scen", 1).astype(F32)
        pieces.append(keep[:columns] + swap(keep[columns:].astype(BF16), "scen", 2).astype(F32))
    live_mask = jnp.arange(width) < size_here
    angles_here = jnp.where(live_mask, jnp.concatenate(pieces, axis=1), 0.0)
    return (angles_here[None], dual_last[None], consensus_last[None])


def solution(mesh):
    spec = P("area", "scen", None)
    return jax.shard_map(
        shards,
        mesh=mesh,
        in_specs=(spec, spec, spec, P(), P(), P()),
        out_specs=(spec, spec, spec),
        check_vma=False,
    )
```

```python
import functools

import jax
import jax.numpy as jnp
from jax import lax
from jax.experimental import pallas as pl
from jax.experimental.pallas import tpu as pltpu
from jax.sharding import PartitionSpec as P


CAP = 128
PENALTY = 1.5
PROXIMAL = 0.5
DENOM = 2.0 * PENALTY + PROXIMAL

F32 = jnp.float32
BF16 = jnp.bfloat16

WHOLE = pl.BlockSpec(memory_space=pltpu.VMEM)
SCALARS = pl.BlockSpec(memory_space=pltpu.SMEM)


def dot_nt(a, b):
    return lax.dot_general(a, b, (((1,), (1,)), ((), ())), preferred_element_type=F32)


def dot_nn(a, b):
    return jnp.dot(a, b, preferred_element_type=F32)


def swap(x, axis, bit):
    n = lax.axis_size(axis)
    return lax.ppermute(x, axis, [(i, i ^ bit) for i in range(n)])


def halves(x):
    high = x.astype(BF16)
    return high, (x - high.astype(F32)).astype(BF16)


def out(shape, dtype):
    return jax.ShapeDtypeStruct(shape, dtype)


def plain_kernel(area_size, injection, dual, packed):
    width = injection.shape[1]
    live = lax.broadcasted_iota(jnp.int32, injection.shape, 1) < area_size[lax.axis_index("area")]
    packed[:, :width] = jnp.where(live, injection[...], 0.0).astype(BF16)
    packed[:, width:] = dual[...].astype(BF16)


def packed_side(area_size, injection, dual):
    return pl.pallas_call(
        plain_kernel,
        out_shape=out((injection.shape[0], injection.shape[1] + dual.shape[1]), BF16),
        in_specs=[SCALARS, WHOLE, WHOLE],
        out_specs=WHOLE,
    )(area_size, injection, dual)


def base_kernel(area_size, near, far, dual, factor, factor_ends, base, keep, send, side, partial):
    step = pl.program_id(0)
    half = near.shape[0]
    block, width = factor.shape

    @pl.when(step == 0)
    def _():
        side[:half] = near[...]
        side[half:] = far[...]
        partial[...] = jnp.zeros_like(partial)

    here = factor_ends[...]
    value = dot_nt(side[:, :width], factor[...])
    start = lax.axis_index("scen") * (pl.num_programs(0) * block) + step * block
    live = start + lax.broadcasted_iota(jnp.int32, value.shape, 1) < area_size[lax.axis_index("area")]
    base[...] = value
    first = jnp.where(live, value - dot_nt(side[:, width:], here), 0.0).astype(BF16)
    partial[...] += dot_nn(first, here)

    @pl.when(step == pl.num_programs(0) - 1)
    def _():
        count = dual.shape[0]
        keep[:count] = PENALTY * partial[:count] + dual[...]
        keep[count:] = PENALTY * partial[count:half]
        send[...] = PENALTY * partial[half:]


def base_product(area_size, near, far, dual, factor, factor_ends):
    rows, width = factor.shape
    half, packed_width = near.shape
    ends_total = factor_ends.shape[1]
    block = 512
    fixed = pl.BlockSpec((half, ends_total), lambda i: (0, 0))
    return pl.pallas_call(
        base_kernel,
        grid=(rows // block,),
        out_shape=(
            out((2 * half, rows), F32),
            out((half, ends_total), F32),
            out((half, ends_total), F32),
        ),
        in_specs=[
            SCALARS,
            WHOLE,
            WHOLE,
            WHOLE,
            pl.BlockSpec((block, width), lambda i: (i, 0)),
            pl.BlockSpec((block, ends_total), lambda i: (i, 0)),
        ],
        out_specs=(pl.BlockSpec((2 * half, block), lambda i: (0, i)), fixed, fixed),
        scratch_shapes=[
            pltpu.VMEM((2 * half, packed_width), BF16),
            pltpu.VMEM((2 * half, ends_total), F32),
        ],
    )(area_size, near, far, dual, factor, factor_ends)


def second_kernel(area_size, base, near, far, factor_ends, second, keep, send, spread):
    half = near.shape[0]
    spread[:half] = near[...]
    spread[half:] = far[...]
    here = factor_ends[...]
    start = lax.axis_index("scen") * here.shape[0]
    live = start + lax.broadcasted_iota(jnp.int32, base.shape, 1) < area_size[lax.axis_index("area")]
    rows = jnp.where(live, base[...] - dot_nt(spread[...], here), 0.0).astype(BF16)
    second[...] = rows
    partial = PENALTY * dot_nn(rows, here)
    keep[...] = partial[:half]
    send[...] = partial[half:]


def second_product(area_size, base, near, far, factor_ends):
    half, ends_total = near.shape
    shape = out((half, ends_total), F32)
    return pl.pallas_call(
        second_kernel,
        out_shape=(out(base.shape, BF16), shape, shape),
        in_specs=[SCALARS, WHOLE, WHOLE, WHOLE, WHOLE],
        out_specs=(WHOLE, WHOLE, WHOLE),
        scratch_shapes=[pltpu.VMEM((2 * half, ends_total), BF16)],
    )(area_size, base, near, far, factor_ends)


def angles_kernel(first_bus, area_size, second, factor, keep, send):
    half, depth = keep.shape
    value = dot_nn(second[...], factor[...])
    start = first_bus + pl.program_id(0) * depth
    live = start + lax.broadcasted_iota(jnp.int32, value.shape, 1) < area_size[lax.axis_index("area")]
    value = jnp.where(live, value, 0.0)
    keep[...] = value[:half]
    send[...] = value[half:].astype(BF16)


def angles_product(area_size, second, factor, parts, part):
    rows, width = factor.shape
    half = second.shape[0] // 2
    depth = 1024
    size = width // parts
    steps = size // depth
    spec = pl.BlockSpec((half, depth), lambda i: (0, i))
    return pl.pallas_call(
        functools.partial(angles_kernel, part * size),
        grid=(steps,),
        out_shape=(out((half, size), F32), out((half, size), BF16)),
        in_specs=[SCALARS, WHOLE, pl.BlockSpec((rows, depth), lambda i: (0, part * steps + i))],
        out_specs=(spec, spec),
    )(area_size, second, factor)


def shards(injection, kkt_factor, dual_price, area_size, bnd_bus, peer_end):
    area_id = lax.axis_index("area")
    areas_all = lax.axis_size("area")
    factor = kkt_factor[0]
    width = factor.shape[1]
    injection_here = injection[0]
    dual_here = dual_price[0]
    columns, ends_total = dual_here.shape
    buses = bnd_bus[area_id]
    peers = peer_end[area_id]
    offset = (peers // ends_total) ^ area_id

    packed = packed_side(area_size, injection_here, dual_here)
    other = swap(packed, "scen", 2)
    pair = jnp.concatenate([packed, other], axis=0)
    pair_far = swap(pair, "scen", 1)

    pick = (jnp.arange(width)[:, None] == buses[None, :]).astype(BF16)
    factor_ends = dot_nn(factor, pick).astype(BF16)
    slots = jnp.arange(ends_total)
    mate = ((slots // CAP * CAP + peers % CAP)[None, :] == slots[:, None]).astype(BF16)

    base, keep, send = base_product(
        area_size, pair, pair_far, dual_here, factor, factor_ends
    )

    def exchange(q):
        moved = q
        bit = 1
        while bit < areas_all:
            moved = jnp.where((offset & bit)[None, :] != 0, swap(moved, "area", bit), moved)
            bit *= 2
        return dot_nn(moved, mate)

    def with_low(x, low_rows):
        high, low = halves(x)
        return jnp.concatenate([high, low[low_rows]], axis=0)

    pair_rows = 2 * columns
    keep = keep + swap(send, "scen", 1)
    pair_rows = 2 * columns
    first_rows, last_rows = slice(0, columns), slice(columns, pair_rows)
    other = swap(with_low(keep, last_rows), "scen", 2).astype(F32)
    q = keep + jnp.concatenate([other[last_rows] + other[pair_rows:], other[first_rows]], axis=0)
    moved = exchange(with_low(q, first_rows))
    moved = jnp.concatenate([moved[first_rows] + moved[pair_rows:], moved[last_rows]], axis=0)
    consensus = (q + moved) / DENOM
    spread = q - 2.0 * PENALTY * consensus
    spread_pair = spread.astype(BF16)
    spread_far = swap(spread_pair, "scen", 1)

    q_own, consensus_own = q[:columns], consensus[:columns]
    second, keep, send = second_product(area_size, base, spread_pair, spread_far, factor_ends)
    far = swap(send, "scen", 1)
    keep = keep + far
    other = swap(with_low(keep[columns:], first_rows), "scen", 2).astype(F32)
    parts = 2
    products = []
    for part in range(parts):
        products.append(angles_product(area_size, second, factor, parts, part))
    q_last = keep[:columns] + other[first_rows] + other[last_rows]
    q_last = q_last + (q_own - PENALTY * consensus_own)
    moved = exchange(with_low(q_last, first_rows))
    moved = moved[first_rows] + moved[last_rows]
    consensus_last = (q_last + moved + PROXIMAL * consensus_own) / DENOM
    dual_last = q_last - PENALTY * consensus_last

    pieces = []
    for keep, send in products:
        keep = keep + swap(send, "scen", 1).astype(F32)
        pieces.append(keep[:columns] + swap(keep[columns:].astype(BF16), "scen", 2).astype(F32))
    angles_here = jnp.concatenate(pieces, axis=1)
    return (angles_here[None], dual_last[None], consensus_last[None])


def solution(mesh):
    spec = P("area", "scen", None)
    return jax.shard_map(
        shards,
        mesh=mesh,
        in_specs=(spec, spec, spec, P(), P(), P()),
        out_specs=(spec, spec, spec),
        check_vma=False,
    )
```

```python
import functools

import jax
import jax.numpy as jnp
from jax import lax
from jax.experimental import pallas as pl
from jax.experimental.pallas import tpu as pltpu
from jax.sharding import PartitionSpec as P


CAP = 128
PENALTY = 1.5
PROXIMAL = 0.5
DENOM = 2.0 * PENALTY + PROXIMAL

F32 = jnp.float32
BF16 = jnp.bfloat16

WHOLE = pl.BlockSpec(memory_space=pltpu.VMEM)
SCALARS = pl.BlockSpec(memory_space=pltpu.SMEM)


def dot_nt(a, b):
    return lax.dot_general(a, b, (((1,), (1,)), ((), ())), preferred_element_type=F32)


def dot_nn(a, b):
    return jnp.dot(a, b, preferred_element_type=F32)


def swap(x, axis, bit):
    n = lax.axis_size(axis)
    return lax.ppermute(x, axis, [(i, i ^ bit) for i in range(n)])


def halves(x):
    high = x.astype(BF16)
    return high, (x - high.astype(F32)).astype(BF16)


def out(shape, dtype):
    return jax.ShapeDtypeStruct(shape, dtype)


def on_chip(x):
    return pltpu.with_memory_space_constraint(x, pltpu.VMEM)


def plain_kernel(area_size, injection, dual, packed):
    width = injection.shape[1]
    live = lax.broadcasted_iota(jnp.int32, injection.shape, 1) < area_size[lax.axis_index("area")]
    packed[:, :width] = jnp.where(live, injection[...], 0.0).astype(BF16)
    packed[:, width:] = dual[...].astype(BF16)


def packed_side(area_size, injection, dual):
    return pl.pallas_call(
        plain_kernel,
        out_shape=out((injection.shape[0], injection.shape[1] + dual.shape[1]), BF16),
        in_specs=[SCALARS, WHOLE, WHOLE],
        out_specs=WHOLE,
    )(area_size, injection, dual)


def base_kernel(
    area_size, near, far, dual, factor, ends_low, ends_high, base, keep, send, side, partial
):
    step = pl.program_id(0)
    half = near.shape[0]
    block, width = factor.shape

    @pl.when(step == 0)
    def _():
        side[:half] = near[...]
        side[half:] = far[...]
        partial[...] = jnp.zeros_like(partial)

    here = jnp.concatenate([ends_low[...], ends_high[...]], axis=1)
    value = dot_nt(side[:, :width], factor[...])
    start = lax.axis_index("scen") * (pl.num_programs(0) * block) + step * block
    live = start + lax.broadcasted_iota(jnp.int32, value.shape, 1) < area_size[lax.axis_index("area")]
    base[...] = value
    first = jnp.where(live, value - dot_nt(side[:, width:], here), 0.0).astype(BF16)
    partial[...] += dot_nn(first, here)

    @pl.when(step == pl.num_programs(0) - 1)
    def _():
        count = dual.shape[0]
        keep[:count] = PENALTY * partial[:count] + dual[...]
        keep[count:] = PENALTY * partial[count:half]
        send[...] = PENALTY * partial[half:]


def base_product(area_size, near, far, dual, factor, factor_ends):
    rows, width = factor.shape
    half, packed_width = near.shape
    ends_total = dual.shape[1]
    block = 512
    fixed = pl.BlockSpec((half, ends_total), lambda i: (0, 0))
    return pl.pallas_call(
        base_kernel,
        grid=(rows // block,),
        out_shape=(
            pltpu.VMEM((2 * half, rows), F32),
            pltpu.VMEM((half, ends_total), F32),
            pltpu.VMEM((half, ends_total), F32),
        ),
        in_specs=[
            SCALARS,
            WHOLE,
            WHOLE,
            WHOLE,
            pl.BlockSpec((block, width), lambda i: (i, 0)),
            pl.BlockSpec((block, ends_total // 2), lambda i: (i, 0)),
            pl.BlockSpec((block, ends_total // 2), lambda i: (i, 0)),
        ],
        out_specs=(pl.BlockSpec((2 * half, block), lambda i: (0, i)), fixed, fixed),
        scratch_shapes=[
            pltpu.VMEM((2 * half, packed_width), BF16),
            pltpu.VMEM((2 * half, ends_total), F32),
        ],
    )(area_size, on_chip(near), on_chip(far), dual, factor, *factor_ends)


def second_kernel(
    area_size, base, near, far, ends_low, ends_high, second, keep, send, spread
):
    half = near.shape[0]
    spread[:half] = near[...]
    spread[half:] = far[...]
    here = jnp.concatenate([ends_low[...], ends_high[...]], axis=1)
    start = lax.axis_index("scen") * here.shape[0]
    live = start + lax.broadcasted_iota(jnp.int32, base.shape, 1) < area_size[lax.axis_index("area")]
    rows = jnp.where(live, base[...] - dot_nt(spread[...], here), 0.0).astype(BF16)
    second[...] = rows
    partial = PENALTY * dot_nn(rows, here)
    keep[...] = partial[:half]
    send[...] = partial[half:]


def second_product(area_size, base, near, far, factor_ends):
    half, ends_total = near.shape
    shape = pltpu.VMEM((half, ends_total), F32)
    return pl.pallas_call(
        second_kernel,
        out_shape=(pltpu.VMEM(base.shape, BF16), shape, shape),
        in_specs=[SCALARS, WHOLE, WHOLE, WHOLE, WHOLE, WHOLE],
        out_specs=(WHOLE, WHOLE, WHOLE),
        scratch_shapes=[pltpu.VMEM((2 * half, ends_total), BF16)],
    )(area_size, *map(on_chip, (base, near, far, *factor_ends)))


def angles_kernel(first_bus, area_size, second, factor, keep, send):
    half, depth = keep.shape
    value = dot_nn(second[...], factor[...])
    start = first_bus + pl.program_id(0) * depth
    live = start + lax.broadcasted_iota(jnp.int32, value.shape, 1) < area_size[lax.axis_index("area")]
    value = jnp.where(live, value, 0.0)
    keep[...] = value[:half]
    send[...] = value[half:].astype(BF16)


def angles_product(area_size, second, factor, parts, part):
    rows, width = factor.shape
    half = second.shape[0] // 2
    depth = 1024
    size = width // parts
    steps = size // depth
    spec = pl.BlockSpec((half, depth), lambda i: (0, i))
    return pl.pallas_call(
        functools.partial(angles_kernel, part * size),
        grid=(steps,),
        out_shape=(out((half, size), F32), out((half, size), BF16)),
        in_specs=[SCALARS, WHOLE, pl.BlockSpec((rows, depth), lambda i: (0, part * steps + i))],
        out_specs=(spec, spec),
    )(area_size, second, factor)


def shards(injection, kkt_factor, dual_price, area_size, bnd_bus, peer_end):
    area_id = lax.axis_index("area")
    areas_all = lax.axis_size("area")
    factor = kkt_factor[0]
    width = factor.shape[1]
    injection_here = injection[0]
    dual_here = dual_price[0]
    columns, ends_total = dual_here.shape
    buses = bnd_bus[area_id]
    peers = peer_end[area_id]
    offset = (peers // ends_total) ^ area_id

    packed = packed_side(area_size, injection_here, dual_here)
    other = swap(packed, "scen", 2)
    pair = jnp.concatenate([packed, other], axis=0)
    pair_far = swap(pair, "scen", 1)

    factor_ends = []
    for chosen in jnp.split(buses, 2):
        pick = (jnp.arange(width)[:, None] == chosen[None, :]).astype(BF16)
        factor_ends.append(dot_nn(factor, pick).astype(BF16))
    slots = jnp.arange(ends_total)
    mate = ((slots // CAP * CAP + peers % CAP)[None, :] == slots[:, None]).astype(BF16)

    base, keep, send = base_product(
        area_size, pair, pair_far, dual_here, factor, factor_ends
    )

    def exchange(q):
        moved = q
        bit = 1
        while bit < areas_all:
            moved = jnp.where((offset & bit)[None, :] != 0, swap(moved, "area", bit), moved)
            bit *= 2
        return dot_nn(moved, mate)

    def with_low(x, low_rows):
        high, low = halves(x)
        return jnp.concatenate([high, low[low_rows]], axis=0)

    pair_rows = 2 * columns
    keep = keep + swap(send, "scen", 1)
    pair_rows = 2 * columns
    first_rows, last_rows = slice(0, columns), slice(columns, pair_rows)
    other = swap(with_low(keep, last_rows), "scen", 2).astype(F32)
    q = keep + jnp.concatenate([other[last_rows] + other[pair_rows:], other[first_rows]], axis=0)
    consensus = (q + exchange(q.astype(BF16))) / DENOM
    spread = q - 2.0 * PENALTY * consensus
    spread_pair = spread.astype(BF16)
    spread_far = swap(spread_pair, "scen", 1)

    q_own, consensus_own = q[:columns], consensus[:columns]
    second, keep, send = second_product(area_size, base, spread_pair, spread_far, factor_ends)
    far = swap(send, "scen", 1)
    keep = keep + far
    other = swap(with_low(keep[columns:], first_rows), "scen", 2).astype(F32)
    parts = 2
    products = []
    for part in range(parts):
        products.append(angles_product(area_size, second, factor, parts, part))
    q_last = keep[:columns] + other[first_rows] + other[last_rows]
    q_last = q_last + (q_own - PENALTY * consensus_own)
    moved = exchange(with_low(q_last, first_rows))
    moved = moved[first_rows] + moved[last_rows]
    consensus_last = (q_last + moved + PROXIMAL * consensus_own) / DENOM
    dual_last = q_last - PENALTY * consensus_last

    pieces = []
    for keep, send in products:
        keep = keep + swap(send, "scen", 1).astype(F32)
        pieces.append(keep[:columns] + swap(keep[columns:].astype(BF16), "scen", 2).astype(F32))
    angles_here = jnp.concatenate(pieces, axis=1)
    return (angles_here[None], dual_last[None], consensus_last[None])


def solution(mesh):
    spec = P("area", "scen", None)
    return jax.shard_map(
        shards,
        mesh=mesh,
        in_specs=(spec, spec, spec, P(), P(), P()),
        out_specs=(spec, spec, spec),
        check_vma=False,
    )
```

```python
import functools

import jax
import jax.numpy as jnp
from jax import lax
from jax.experimental import pallas as pl
from jax.experimental.pallas import tpu as pltpu
from jax.sharding import PartitionSpec as P


CAP = 128
PENALTY = 1.5
PROXIMAL = 0.5
DENOM = 2.0 * PENALTY + PROXIMAL

F32 = jnp.float32
BF16 = jnp.bfloat16

WHOLE = pl.BlockSpec(memory_space=pltpu.VMEM)
SCALARS = pl.BlockSpec(memory_space=pltpu.SMEM)


def dot_nt(a, b):
    return lax.dot_general(a, b, (((1,), (1,)), ((), ())), preferred_element_type=F32)


def dot_nn(a, b):
    return jnp.dot(a, b, preferred_element_type=F32)


def swap(x, axis, bit):
    n = lax.axis_size(axis)
    return lax.ppermute(x, axis, [(i, i ^ bit) for i in range(n)])


def halves(x):
    high = x.astype(BF16)
    return high, (x - high.astype(F32)).astype(BF16)


def room(mebibytes):
    return pltpu.CompilerParams(vmem_limit_bytes=mebibytes * 2**20)


def on_chip(x):
    return pltpu.with_memory_space_constraint(x, pltpu.VMEM)


def plain_kernel(area_size, injection, dual, packed):
    width = injection.shape[1]
    live = lax.broadcasted_iota(jnp.int32, injection.shape, 1) < area_size[lax.axis_index("area")]
    packed[:, :width] = jnp.where(live, injection[...], 0.0).astype(BF16)
    packed[:, width:] = dual[...].astype(BF16)


def packed_side(area_size, injection, dual):
    return pl.pallas_call(
        plain_kernel,
        out_shape=pltpu.VMEM((injection.shape[0], injection.shape[1] + dual.shape[1]), BF16),
        in_specs=[SCALARS, WHOLE, WHOLE],
        out_specs=WHOLE,
        compiler_params=room(4),
    )(area_size, injection, dual)


def base_kernel(area_size, near, far, dual, factor, factor_ends, base, keep, send, side, partial):
    step = pl.program_id(0)
    half = near.shape[0]
    block, width = factor.shape

    @pl.when(step == 0)
    def _():
        side[:half] = near[...]
        side[half:] = far[...]
        partial[...] = jnp.zeros_like(partial)

    here = factor_ends[pl.ds(pl.multiple_of(step * block, block), block), :]
    value = dot_nt(side[:, :width], factor[...])
    start = lax.axis_index("scen") * (pl.num_programs(0) * block) + step * block
    live = start + lax.broadcasted_iota(jnp.int32, value.shape, 1) < area_size[lax.axis_index("area")]
    base[...] = value
    first = jnp.where(live, value - dot_nt(side[:, width:], here), 0.0).astype(BF16)
    partial[...] += dot_nn(first, here)

    @pl.when(step == pl.num_programs(0) - 1)
    def _():
        count = dual.shape[0]
        keep[:count] = PENALTY * partial[:count] + dual[...]
        keep[count:] = PENALTY * partial[count:half]
        send[...] = PENALTY * partial[half:]


def base_product(area_size, near, far, dual, factor, factor_ends):
    rows, width = factor.shape
    half, packed_width = near.shape
    ends_total = dual.shape[1]
    block = 512
    fixed = pl.BlockSpec((half, ends_total), lambda i: (0, 0))
    return pl.pallas_call(
        base_kernel,
        grid=(rows // block,),
        out_shape=(
            pltpu.VMEM((2 * half, rows), F32),
            pltpu.VMEM((half, ends_total), F32),
            pltpu.VMEM((half, ends_total), F32),
        ),
        in_specs=[
            SCALARS,
            WHOLE,
            WHOLE,
            WHOLE,
            pl.BlockSpec((block, width), lambda i: (i, 0)),
            WHOLE,
        ],
        out_specs=(pl.BlockSpec((2 * half, block), lambda i: (0, i)), fixed, fixed),
        scratch_shapes=[
            pltpu.VMEM((2 * half, packed_width), BF16),
            pltpu.VMEM((2 * half, ends_total), F32),
        ],
        compiler_params=room(24),
    )(area_size, on_chip(near), on_chip(far), dual, factor, on_chip(factor_ends))


def second_kernel(area_size, base, near, far, factor_ends, second, keep, send, spread):
    half = near.shape[0]
    spread[:half] = near[...]
    spread[half:] = far[...]
    here = factor_ends[...]
    start = lax.axis_index("scen") * here.shape[0]
    live = start + lax.broadcasted_iota(jnp.int32, base.shape, 1) < area_size[lax.axis_index("area")]
    rows = jnp.where(live, base[...] - dot_nt(spread[...], here), 0.0).astype(BF16)
    second[...] = rows
    partial = PENALTY * dot_nn(rows, here)
    keep[...] = partial[:half]
    send[...] = partial[half:]


def second_product(area_size, base, near, far, factor_ends):
    half, ends_total = near.shape
    shape = pltpu.VMEM((half, ends_total), F32)
    return pl.pallas_call(
        second_kernel,
        out_shape=(pltpu.VMEM(base.shape, BF16), shape, shape),
        in_specs=[SCALARS, WHOLE, WHOLE, WHOLE, WHOLE],
        out_specs=(WHOLE, WHOLE, WHOLE),
        scratch_shapes=[pltpu.VMEM((2 * half, ends_total), BF16)],
        compiler_params=room(8),
    )(area_size, *map(on_chip, (base, near, far, factor_ends)))


def angles_kernel(first_bus, area_size, second, factor, keep, send):
    half, depth = keep.shape
    value = dot_nn(second[...], factor[...])
    start = first_bus + pl.program_id(0) * depth
    live = start + lax.broadcasted_iota(jnp.int32, value.shape, 1) < area_size[lax.axis_index("area")]
    value = jnp.where(live, value, 0.0)
    keep[...] = value[:half]
    send[...] = value[half:].astype(BF16)


def angles_product(area_size, second, factor, parts, part):
    rows, width = factor.shape
    half = second.shape[0] // 2
    depth = 1024
    size = width // parts
    steps = size // depth
    spec = pl.BlockSpec((half, depth), lambda i: (0, i))
    return pl.pallas_call(
        functools.partial(angles_kernel, part * size),
        grid=(steps,),
        out_shape=(pltpu.VMEM((half, size), F32), pltpu.VMEM((half, size), BF16)),
        in_specs=[SCALARS, WHOLE, pl.BlockSpec((rows, depth), lambda i: (0, part * steps + i))],
        out_specs=(spec, spec),
        compiler_params=room(14),
    )(area_size, on_chip(second), factor)


def shards(injection, kkt_factor, dual_price, area_size, bnd_bus, peer_end):
    area_id = lax.axis_index("area")
    areas_all = lax.axis_size("area")
    factor = kkt_factor[0]
    width = factor.shape[1]
    injection_here = injection[0]
    dual_here = dual_price[0]
    columns, ends_total = dual_here.shape
    buses = bnd_bus[area_id]
    peers = peer_end[area_id]
    offset = (peers // ends_total) ^ area_id

    packed = packed_side(area_size, injection_here, dual_here)
    other = swap(packed, "scen", 2)
    pair = jnp.concatenate([packed, other], axis=0)
    pair_far = swap(pair, "scen", 1)

    pick = (jnp.arange(width)[:, None] == buses[None, :]).astype(BF16)
    factor_ends = dot_nn(factor, pick).astype(BF16)
    slots = jnp.arange(ends_total)
    mate = ((slots // CAP * CAP + peers % CAP)[None, :] == slots[:, None]).astype(BF16)

    base, keep, send = base_product(
        area_size, pair, pair_far, dual_here, factor, factor_ends
    )

    def exchange(q):
        moved = q
        bit = 1
        while bit < areas_all:
            moved = jnp.where((offset & bit)[None, :] != 0, swap(moved, "area", bit), moved)
            bit *= 2
        return dot_nn(moved, mate)

    def with_low(x, low_rows):
        high, low = halves(x)
        return jnp.concatenate([high, low[low_rows]], axis=0)

    pair_rows = 2 * columns
    keep = keep + swap(send, "scen", 1)
    pair_rows = 2 * columns
    first_rows, last_rows = slice(0, columns), slice(columns, pair_rows)
    other = swap(with_low(keep, last_rows), "scen", 2).astype(F32)
    q = keep + jnp.concatenate([other[last_rows] + other[pair_rows:], other[first_rows]], axis=0)
    consensus = (q + exchange(q.astype(BF16))) / DENOM
    spread = q - 2.0 * PENALTY * consensus
    spread_pair = spread.astype(BF16)
    spread_far = swap(spread_pair, "scen", 1)

    q_own, consensus_own = q[:columns], consensus[:columns]
    second, keep, send = second_product(area_size, base, spread_pair, spread_far, factor_ends)
    far = swap(send, "scen", 1)
    keep = keep + far
    other = swap(with_low(keep[columns:], first_rows), "scen", 2).astype(F32)
    parts = 2
    products = []
    for part in range(parts):
        products.append(angles_product(area_size, second, factor, parts, part))
    q_last = keep[:columns] + other[first_rows] + other[last_rows]
    q_last = q_last + (q_own - PENALTY * consensus_own)
    moved = exchange(with_low(q_last, first_rows))
    moved = moved[first_rows] + moved[last_rows]
    consensus_last = (q_last + moved + PROXIMAL * consensus_own) / DENOM
    dual_last = q_last - PENALTY * consensus_last

    pieces = []
    for keep, send in products:
        keep = keep + swap(send, "scen", 1).astype(F32)
        pieces.append(keep[:columns] + swap(keep[columns:].astype(BF16), "scen", 2).astype(F32))
    angles_here = jnp.concatenate(pieces, axis=1)
    return (angles_here[None], dual_last[None], consensus_last[None])


def solution(mesh):
    spec = P("area", "scen", None)
    return jax.shard_map(
        shards,
        mesh=mesh,
        in_specs=(spec, spec, spec, P(), P(), P()),
        out_specs=(spec, spec, spec),
        check_vma=False,
    )
```

```python
import functools

import jax
import jax.numpy as jnp
from jax import lax
from jax.experimental import pallas as pl
from jax.experimental.pallas import tpu as pltpu
from jax.sharding import PartitionSpec as P


CAP = 128
PENALTY = 1.5
PROXIMAL = 0.5
DENOM = 2.0 * PENALTY + PROXIMAL

F32 = jnp.float32
BF16 = jnp.bfloat16

WHOLE = pl.BlockSpec(memory_space=pltpu.VMEM)
SCALARS = pl.BlockSpec(memory_space=pltpu.SMEM)


def dot_nt(a, b):
    return lax.dot_general(a, b, (((1,), (1,)), ((), ())), preferred_element_type=F32)


def dot_nn(a, b):
    return jnp.dot(a, b, preferred_element_type=F32)


def swap(x, axis, bit):
    n = lax.axis_size(axis)
    return lax.ppermute(x, axis, [(i, i ^ bit) for i in range(n)])


def halves(x):
    high = x.astype(BF16)
    return high, (x - high.astype(F32)).astype(BF16)


def room(mebibytes):
    return pltpu.CompilerParams(vmem_limit_bytes=mebibytes * 2**20)


def off_chip(x):
    return pltpu.with_memory_space_constraint(x, pltpu.HBM)


def on_chip(x):
    return pltpu.with_memory_space_constraint(x, pltpu.VMEM)


def plain_kernel(area_size, injection, dual, packed):
    width = injection.shape[1]
    live = lax.broadcasted_iota(jnp.int32, injection.shape, 1) < area_size[lax.axis_index("area")]
    packed[:, :width] = jnp.where(live, injection[...], 0.0).astype(BF16)
    packed[:, width:] = dual[...].astype(BF16)


def packed_side(area_size, injection, dual):
    return pl.pallas_call(
        plain_kernel,
        out_shape=pltpu.VMEM((injection.shape[0], injection.shape[1] + dual.shape[1]), BF16),
        in_specs=[SCALARS, WHOLE, WHOLE],
        out_specs=WHOLE,
        compiler_params=room(4),
    )(area_size, off_chip(injection), off_chip(dual))


def base_kernel(
    area_size, near, far, dual, factor, ends_top, ends_bottom, base, keep, send, side, partial
):
    half = near.shape[0]
    count = dual.shape[0]
    rows, width = factor.shape
    block = rows // 2
    side[:half] = near[...]
    side[half:] = far[...]
    for part, ends in enumerate((ends_top, ends_bottom)):
        here = slice(part * block, (part + 1) * block)
        value = dot_nt(side[:, :width], factor[here, :])
        base[:, here] = value
        start = lax.axis_index("scen") * rows + part * block
        live = start + lax.broadcasted_iota(jnp.int32, value.shape, 1) < area_size[
            lax.axis_index("area")
        ]
        first = value - dot_nt(side[:, width:], ends[...])
        ends_part = dot_nn(jnp.where(live, first, 0.0).astype(BF16), ends[...])
        if part:
            ends_part = ends_part + partial[...]
        partial[...] = ends_part
    keep[:count] = PENALTY * partial[:count] + dual[...]
    keep[count:] = PENALTY * partial[count:half]
    send[...] = PENALTY * partial[half:]


def base_product(area_size, near, far, dual, factor, factor_ends):
    rows = factor.shape[0]
    half, packed_width = near.shape
    ends_total = dual.shape[1]
    return pl.pallas_call(
        base_kernel,
        out_shape=(
            pltpu.VMEM((2 * half, rows), F32),
            pltpu.VMEM((half, ends_total), F32),
            pltpu.VMEM((half, ends_total), F32),
        ),
        in_specs=[SCALARS] + [WHOLE] * 6,
        out_specs=(WHOLE, WHOLE, WHOLE),
        scratch_shapes=[
            pltpu.VMEM((2 * half, packed_width), BF16),
            pltpu.VMEM((2 * half, ends_total), F32),
        ],
        compiler_params=room(24),
    )(area_size, *map(on_chip, (near, far, dual, factor, *factor_ends)))


def second_kernel(
    area_size, base, near, far, ends_top, ends_bottom, second, keep, send, spread
):
    half = near.shape[0]
    spread[:half] = near[...]
    spread[half:] = far[...]
    rows = base.shape[1]
    block = rows // 2
    partial = None
    for part, ends in enumerate((ends_top, ends_bottom)):
        here = slice(part * block, (part + 1) * block)
        value = base[:, here] - dot_nt(spread[...], ends[...])
        start = lax.axis_index("scen") * rows + part * block
        live = start + lax.broadcasted_iota(jnp.int32, value.shape, 1) < area_size[
            lax.axis_index("area")
        ]
        value = jnp.where(live, value, 0.0).astype(BF16)
        second[:, here] = value
        ends_part = PENALTY * dot_nn(value, ends[...])
        partial = ends_part if partial is None else partial + ends_part
    keep[...] = partial[:half]
    send[...] = partial[half:]


def second_product(area_size, base, near, far, factor_ends):
    half, ends_total = near.shape
    shape = pltpu.VMEM((half, ends_total), F32)
    return pl.pallas_call(
        second_kernel,
        out_shape=(pltpu.VMEM(base.shape, BF16), shape, shape),
        in_specs=[SCALARS] + [WHOLE] * 5,
        out_specs=(WHOLE, WHOLE, WHOLE),
        scratch_shapes=[pltpu.VMEM((2 * half, ends_total), BF16)],
        compiler_params=room(8),
    )(area_size, *map(on_chip, (base, near, far, *factor_ends)))


def angles_kernel(first_bus, area_size, second, factor, keep, send):
    half, size = keep.shape
    depth = 512
    for start in range(0, size, depth):
        here = slice(start, start + depth)
        buses = slice(first_bus + start, first_bus + start + depth)
        value = dot_nn(second[...], factor[:, buses])
        bus = buses.start + lax.broadcasted_iota(jnp.int32, value.shape, 1)
        value = jnp.where(bus < area_size[lax.axis_index("area")], value, 0.0)
        keep[:, here] = value[:half]
        send[:, here] = value[half:].astype(BF16)


def angles_product(area_size, second, factor, parts, part):
    half = second.shape[0] // 2
    size = factor.shape[1] // parts
    return pl.pallas_call(
        functools.partial(angles_kernel, part * size),
        out_shape=(pltpu.VMEM((half, size), F32), pltpu.VMEM((half, size), BF16)),
        in_specs=[SCALARS, WHOLE, WHOLE],
        out_specs=(WHOLE, WHOLE),
        compiler_params=room(14),
    )(area_size, on_chip(second), on_chip(factor))


def shards(injection, kkt_factor, dual_price, area_size, bnd_bus, peer_end):
    area_id = lax.axis_index("area")
    areas_all = lax.axis_size("area")
    factor = kkt_factor[0]
    width = factor.shape[1]
    injection_here = injection[0]
    dual_here = dual_price[0]
    columns, ends_total = dual_here.shape
    buses = bnd_bus[area_id]
    peers = peer_end[area_id]
    offset = (peers // ends_total) ^ area_id

    packed = packed_side(area_size, injection_here, dual_here)
    other = swap(packed, "scen", 2)
    pair = jnp.concatenate([packed, other], axis=0)
    pair_far = swap(pair, "scen", 1)

    pick = (jnp.arange(width)[:, None] == buses[None, :]).astype(BF16)
    factor_ends = []
    for rows in jnp.split(factor, 2, axis=0):
        factor_ends.append(dot_nn(rows, pick).astype(BF16))
    slots = jnp.arange(ends_total)
    mate = ((slots // CAP * CAP + peers % CAP)[None, :] == slots[:, None]).astype(BF16)

    base, keep, send = base_product(
        area_size, pair, pair_far, dual_here, factor, factor_ends
    )

    def exchange(q):
        moved = q
        for hop in range(areas_all.bit_length() - 1):
            bit = 1 << hop
            other = swap(moved, "area", bit)
            moved = jnp.where((offset & bit)[None, :] != 0, other, moved)
        return dot_nn(moved, mate)

    def with_low(x, low_rows):
        high, low = halves(x)
        return jnp.concatenate([high, low[low_rows]], axis=0)

    pair_rows = 2 * columns
    keep = keep + swap(send, "scen", 1)
    pair_rows = 2 * columns
    first_rows, last_rows = slice(0, columns), slice(columns, pair_rows)
    other = swap(with_low(keep, last_rows), "scen", 2).astype(F32)
    q = keep + jnp.concatenate([other[last_rows] + other[pair_rows:], other[first_rows]], axis=0)
    consensus = (q + exchange(q.astype(BF16))) / DENOM
    spread = q - 2.0 * PENALTY * consensus
    spread_pair = spread.astype(BF16)
    spread_far = swap(spread_pair, "scen", 1)

    q_own, consensus_own = q[:columns], consensus[:columns]
    second, keep, send = second_product(area_size, base, spread_pair, spread_far, factor_ends)
    far = swap(send, "scen", 1)
    keep = keep + far
    other = swap(with_low(keep[columns:], first_rows), "scen", 2).astype(F32)
    parts = 2
    products = []
    for part in range(parts):
        products.append(angles_product(area_size, second, factor, parts, part))
    q_last = keep[:columns] + other[first_rows] + other[last_rows]
    q_last = q_last + (q_own - PENALTY * consensus_own)
    moved = exchange(with_low(q_last, first_rows))
    moved = moved[first_rows] + moved[last_rows]
    consensus_last = (q_last + moved + PROXIMAL * consensus_own) / DENOM
    dual_last = q_last - PENALTY * consensus_last

    pieces = []
    for keep, send in products:
        other = swap(send, "scen", 1)
        keep = keep + other.astype(F32)
        sent = keep[columns:].astype(BF16)
        other = swap(sent, "scen", 2)
        pieces.append(keep[:columns] + other.astype(F32))
    angles_here = jnp.concatenate(pieces, axis=1)[None]
    return (angles_here, dual_last[None], consensus_last[None])


def solution(mesh):
    spec = P("area", "scen", None)
    return jax.shard_map(
        shards,
        mesh=mesh,
        in_specs=(spec, spec, spec, P(), P(), P()),
        out_specs=(spec, spec, spec),
        check_vma=False,
    )
```
